256 devices in a mesh: bins: 64 (over z, y, x_hi), det: 4 (over x_lo, core).
Axes of the slice: x: 4 (x_hi: 2, x_lo: 2; x = x_hi * 2 + x_lo), y: 4, z: 8, core: 2. Of those that a mesh axis runs over, the one named last changes fastest.
Arguments:
- strain: float32 [4, 17408], P('det', 'bins'), may hold values from -6 to 6
- filters: bfloat16 [64, 512, 1024], P('bins'), may hold values from -0.1875 to 0.1875
- mixing: bfloat16 [64, 2, 256, 512], P('bins'), may hold values from -0.375 to 0.375
- counts: int32 [64], P('bins'), may hold values from 64 to 512
- rate_bands: int32 [64], P('bins'), may hold values from 0 to 4
Outputs:
- network_power: float32 [64, 256, 512], P('bins', 'det')
The draws below stay inside these ranges and needn't reach their ends.
All inputs are finite; a program needn't handle non-finite values.
Results may differ from the reference program's by a relative error of at most 0.0032.
Values may be sent and summed in bfloat16 or wider, within the bound.
A program may use at most 64 MiB of HBM per device.

```python
from functools import partial
import jax
import jax.numpy as jnp
from jax import lax

N_DETECTORS = 4
NBINS = 64
KMAX = 512
TAPS = 1024
TPL = 256
OUT0 = 512
RATES = 5
SAMPLES = 17408


def plant(values, rng, least, top_value):
    longest = values.shape.index(max(values.shape))
    spots = []
    for shift in (0, 1):
        where = [jax.random.randint(jax.random.fold_in(rng, axis), (), 0, length) for axis, length in enumerate(values.shape)]
        where[longest] = (where[longest] + shift) % values.shape[longest]
        spots.append(tuple(where))
    return values.at[spots[0]].set(least).at[spots[1]].set(top_value)


def steps_of(own_key, dims, shards, least, high):
    def one(position, blocks):
        heights = jax.random.uniform(jax.random.fold_in(jax.random.fold_in(own_key, 6), position), (blocks,), jnp.float32, least / len(shards), high / len(shards))
        return jnp.repeat(jnp.exp(heights), dims[position] // blocks).reshape((-1,) + (1,) * (len(dims) - position - 1))

    loudness = one(*shards[0])
    for cut in shards[1:]:
        loudness = loudness * one(*cut)
    return loudness


def noise(rng, dims, spread, reach, shards=(), dtype=jnp.bfloat16):
    result = jax.random.normal(rng, dims, jnp.float32) * spread
    if len(shards) > 0:
        result = steps_of(rng, dims, shards, -0.22, 0.18) * result
    return jnp.clip(result, min=-reach, max=reach).astype(dtype)


def setup_inputs(seed: int = 0) -> dict:
    streams_of = jax.random.split(jax.random.key(seed), 6)
    strain = noise(streams_of[0], (N_DETECTORS, SAMPLES), 1.0, 6.0, ((0, 4), (1, 64)), jnp.float32)
    filters = noise(streams_of[1], (NBINS, KMAX, TAPS), TAPS ** -0.5, 0.1875, ((0, 64),))
    mixing = noise(streams_of[2], (NBINS, 2, TPL, KMAX), (KMAX // 2) ** -0.5, 0.375, ((0, 64),))
    counts = plant(jax.random.randint(streams_of[3], (NBINS,), KMAX // 8, min(KMAX, 2 * TPL) + 1), jax.random.fold_in(streams_of[3], 1), KMAX // 8, min(KMAX, 2 * TPL)).astype(jnp.int32)
    rate_bands = plant(jax.random.randint(streams_of[4], (NBINS,), 0, RATES), jax.random.fold_in(streams_of[4], 1), 0, RATES - 1).astype(jnp.int32)
    return dict(strain=strain, filters=filters, mixing=mixing, counts=counts, rate_bands=rate_bands)


def decimate(series):
    return 0.5 * jnp.sum(series.reshape(-1, 2), axis=1)


def ladder(series):
    levels = [series]
    for rate_index in range(RATES - 1):
        levels.append(decimate(levels[-1]))
    return levels


def power_rate(rate_index, levels, filter_bank, mixing, live_count):
    series = levels[rate_index]
    taps = filter_bank.shape[1]
    out_len = OUT0 >> rate_index
    offset = series.shape[0] - out_len - taps + 1
    segment = series[offset:].astype(jnp.bfloat16)
    basis_snr = lax.conv_general_dilated(segment[None, None, :], filter_bank[:, None, :], (1,), "VALID", preferred_element_type=jnp.float32)[0]
    live_rows = jnp.arange(filter_bank.shape[0]) < live_count
    basis_snr = jnp.where(live_rows[:, None], basis_snr, 0.0).astype(jnp.bfloat16)
    rows = mixing.shape[1]
    template_snr = jnp.dot(mixing.reshape(2 * rows, -1), basis_snr, preferred_element_type=jnp.float32)
    power_sum = template_snr[:rows] * template_snr[:rows] + template_snr[rows:] * template_snr[rows:]
    return jnp.repeat(power_sum, 1 << rate_index, axis=1)


def detector_power(series, filters, mixing, counts, rate_bands):
    levels = ladder(series)
    branches = [partial(power_rate, rate_index, levels) for rate_index in range(RATES)]

    def one_bin(items):
        return lax.switch(items[3], branches, items[0], items[1], items[2])

    return lax.map(one_bin, (filters, mixing, counts, rate_bands))


def reference(strain, filters, mixing, counts, rate_bands):
    network_power = jnp.zeros((filters.shape[0], mixing.shape[2], OUT0), jnp.float32)
    for detector in range(N_DETECTORS):
        network_power = network_power + detector_power(strain[detector], filters, mixing, counts, rate_bands)
    return network_power
```

```python
import jax
import jax.numpy as jnp
from jax import lax
from jax.experimental import pallas as pl
from jax.experimental.pallas import tpu as pltpu
from jax.sharding import PartitionSpec as P

DETS = 4
KMAX = 512
TAPS = 1024
TPL = 256
OUT0 = 512
SAMPLES = 17408
SHARD = 272
NZ, NY, NX = 8, 4, 2
NE = NX * DETS
PART = TPL // DETS
LANES = 128
MESH = pl.DeviceIdType.MESH
F32 = jnp.float32
BF16 = jnp.bfloat16
WIDTH = (272, 136, 68, 34, 17)
COLUMN = (0, 0, 136, 204, 238)
START = tuple((SAMPLES >> r) - (OUT0 >> r) - (TAPS - 1) for r in range(5))


def iota(shape, dim):
    return lax.broadcasted_iota(jnp.int32, shape, dim)


def ladder_matrix():
    col = iota((1, 2 * LANES), 1)
    sample = iota((3 * LANES, 2 * LANES), 0)
    matrix = jnp.zeros((3 * LANES, 2 * LANES), F32)
    for r in range(1, 5):
        here = (col >= COLUMN[r]) & (col < COLUMN[r] + WIDTH[r])
        matrix = jnp.where(here & ((sample >> r) == col - COLUMN[r]), 0.5**r, matrix)
    return matrix.astype(BF16)


def gather_kernel(
    counts_ref,
    strain_ref,
    filters_ref,
    mixing_ref,
    seen_ref,
    bank_ref,
    padded,
    column,
    filters,
    mixing,
    local_sem,
    zs,
    zr,
    ys,
    yr,
    es,
    er,
):
    at_bin = lax.axis_index("bins")
    det = lax.axis_index("det")
    z = at_bin // (NY * NX)
    y = (at_bin // NX) % NY
    xh = at_bin % NX
    e = xh * DETS + det

    def bin_of(z, y, xh):
        return (z * NY + y) * NX + xh

    z_peers = [(bin_of((z + k) % NZ, y, xh), det) for k in range(1, NZ)]
    y_peers = [(bin_of(z, (y + k) % NY, xh), det) for k in range(1, NY)]
    e_peers = []
    for k in range(1, NE):
        other = (e + k) % NE
        e_peers.append((bin_of(z, y, other // DETS), other % DETS))

    barrier = pltpu.get_barrier_semaphore()
    for peer in z_peers + y_peers + e_peers:
        pl.semaphore_signal(barrier, inc=1, device_id=peer, device_id_type=MESH)

    load_filters = pltpu.make_async_copy(filters_ref, filters, local_sem.at[0])
    load_filters.start()
    rows = pl.ds(pl.multiple_of(det * PART, PART), PART)
    load_mixing = pltpu.make_async_copy(mixing_ref.at[:, :, rows, :], mixing, local_sem.at[1])
    load_mixing.start()

    padded[...] = jnp.zeros_like(padded)
    padded[:, 0:SHARD] = strain_ref[...]
    samples = padded[...]
    high = samples.astype(BF16).astype(F32)
    middle = (samples - high).astype(BF16).astype(F32)
    low = samples - high - middle
    part = iota((8, 3 * LANES), 0)
    wide = [jnp.broadcast_to(p, (8, 3 * LANES)) for p in (high, middle, low)]
    parts = jnp.where(
        part == 0, wide[0], jnp.where(part == 1, wide[1], jnp.where(part == 2, wide[2], 0.0))
    )
    split = jnp.dot(parts.astype(BF16), ladder_matrix(), preferred_element_type=F32)
    ladder = jnp.sum(split, axis=0, keepdims=True)
    row = iota((8, LANES), 0)
    tile = jnp.zeros((8, LANES), F32)
    lines = [ladder[:, :LANES], ladder[:, LANES:]]
    lines += [samples[:, k * LANES : (k + 1) * LANES] for k in range(3)]
    for k, line in enumerate(lines):
        tile = jnp.where(row == k, jnp.broadcast_to(line, (8, LANES)), tile)
    own = pl.ds(pl.multiple_of(z * 8, 8), 8)
    column[own, :] = tile

    pl.semaphore_wait(barrier, NZ + NY + NE - 3)

    def send(ref, send_sem, recv_sem, peer):
        copy = pltpu.make_async_remote_copy(
            src_ref=ref,
            dst_ref=ref,
            send_sem=send_sem,
            recv_sem=recv_sem,
            device_id=peer,
            device_id_type=MESH,
        )
        copy.start()
        return copy

    z_copies = [send(column.at[own, :], zs.at[k], zr.at[k], p) for k, p in enumerate(z_peers)]

    load_mixing.wait()
    live = iota((1, KMAX), 1) < counts_ref[0]
    load_filters.wait()
    mixed = mixing[...].reshape(2 * PART, KMAX)
    mixed = jnp.where(live, mixed, jnp.zeros_like(mixed))
    bank = jnp.dot(mixed, filters[0], preferred_element_type=F32)
    bank = bank.astype(BF16)
    square = (LANES, LANES)
    turn = (iota(square, 0) + iota(square, 1) == LANES - 1).astype(F32).astype(BF16)
    for a in range(TAPS // LANES):
        taps = slice(a * LANES, (a + 1) * LANES)
        bank_ref[:, taps] = jnp.dot(bank[:, taps], turn, preferred_element_type=F32).astype(BF16)

    for copy in z_copies:
        copy.wait_recv()
    low_rows = column[pl.ds(1, 8, stride=8), :]
    last = column[8 * (NZ - 1) : 8 * NZ, :]
    before = column[8 * (NZ - 2) : 8 * (NZ - 1), :]
    high_rows = jnp.where(row == 5, jnp.broadcast_to(before[0:1], (8, LANES)), last)
    seen_ref[e, y] = jnp.concatenate([low_rows, high_rows], axis=0).astype(BF16)

    y_copies = [send(seen_ref.at[e, y], ys.at[k], yr.at[k], p) for k, p in enumerate(y_peers)]
    for copy in y_copies:
        copy.wait_recv()
    e_copies = [send(seen_ref.at[e], es.at[k], er.at[k], p) for k, p in enumerate(e_peers)]
    for copy in e_copies:
        copy.wait_recv()
    for copy in z_copies + y_copies + e_copies:
        copy.wait_send()


def flatten(r, seen_ref, flat):
    lane = iota((8, LANES), 1)
    row = iota((8, LANES), 0)
    halves = {4: "low", 3: "low", 2: "low", 1: "both", 0: "high"}[r]
    width = WIDTH[r]
    picks = []
    moved = [[] for _ in range(DETS)]
    out_row16 = iota((16, 8), 0)
    for y in range(NY):
        for xh in range(NX):
            j = y * NX + xh
            jobs = []
            if halves == "low":
                first = COLUMN[r] - LANES
                jobs.append((0, [8 * z + j for z in range(8)], 0, first, [width] * 8))
            if halves == "both":
                jobs.append((0, [8 * z + j for z in range(8)], LANES, 0, [8] * 8))
                jobs.append(
                    (1, [8 * 7 + j, 0, 0, 0, 0, 8 * 6 + j, 0, 0], 0, 0, [LANES, 0, 0, 0, 0, LANES, 0, 0])
                )
            if halves == "high":
                jobs.append((1, [8 * 7 + j] * 8, None, 0, [0, 0, LANES, LANES, 16, 0, 0, 0]))
            for half, shards, skip, first, widths in jobs:
                begin, shift = [], []
                for k in range(8):
                    extra = (k - 2) * LANES if skip is None else skip
                    at = width * shards[k] + extra - START[r]
                    begin.append(at)
                    shift.append((at - first) % LANES)
                stride = (shift[1] - shift[0]) % LANES
                if any((shift[k] - shift[0] - k * stride) % LANES for k in range(8)):
                    stride = None
                begin_row = jnp.zeros((8, LANES), jnp.int32)
                begin_col = jnp.zeros((16, 8), jnp.int32)
                wide = jnp.zeros((8, LANES), jnp.int32)
                for k in range(8):
                    begin_row = jnp.where(row == k, begin[k], begin_row)
                    begin_col = jnp.where(iota((16, 8), 1) == k, begin[k], begin_col)
                    wide = jnp.where(row == k, widths[k], wide)
                offset = (lane - begin_row) & (LANES - 1)
                wraps = ((begin_row & (LANES - 1)) + offset) >= LANES
                for wrap in (False, True):
                    picks.append((begin_col >> 7) + int(wrap) == out_row16)
                for d in range(DETS):
                    block = seen_ref[xh * DETS + d, y].astype(F32)[8 * half : 8 * half + 8]
                    if stride is None:
                        turned = jnp.zeros((8, LANES), F32)
                        for amount in sorted(set(s for s, w in zip(shift, widths) if w)):
                            rolled = pltpu.roll(block, amount, 1)
                            mask = jnp.zeros((8, LANES), jnp.bool_)
                            for k in range(8):
                                if shift[k] == amount:
                                    mask = mask | (row == k)
                            turned = jnp.where(mask, rolled, turned)
                    elif stride == 0:
                        turned = pltpu.roll(block, shift[0], 1)
                    else:
                        turned = pltpu.roll(block, shift[0], 1)
                        step = min(stride, 16)
                        for _ in range(stride // step):
                            turned = pltpu.roll(turned, 0, 1, stride=step, stride_axis=0)
                    for wrap in (False, True):
                        keep = (offset < wide) & (wraps == wrap)
                        moved[d].append(jnp.where(keep, turned, 0.0))
    pick = jnp.concatenate([p.astype(F32) for p in picks], axis=1).astype(BF16)
    for d in range(DETS):
        data = jnp.concatenate(moved[d], axis=0).astype(BF16)
        flat[:, d * LANES : (d + 1) * LANES] = jnp.dot(pick, data, preferred_element_type=F32)


def filter_kernel(rates_ref, seen_ref, bank_ref, out_ref, flat, hankel):
    rate = rates_ref[0]
    for r in range(5):

        @pl.when(rate == r)
        def _(r=r):
            flatten(r, seen_ref, flat)

    square = (LANES, LANES)
    later = iota(square, 1) > iota(square, 0)
    blocks = OUT0 // LANES + TAPS // LANES - 1
    for d in range(DETS):
        cols = slice(d * LANES, (d + 1) * LANES)
        turned = None
        for m in range(blocks + 1):
            line = jnp.broadcast_to(flat[m : m + 1, cols], square)
            following = pltpu.roll(line, 1, 1, stride=1, stride_axis=0)
            if m:
                hankel[(m - 1) * LANES : m * LANES, cols] = jnp.where(
                    later, following, turned
                ).astype(BF16)
            turned = following

    def power(c):
        snr = jnp.dot(
            bank_ref[...], hankel[c * LANES : c * LANES + TAPS, :], preferred_element_type=F32
        )
        each = snr[:PART] * snr[:PART] + snr[PART:] * snr[PART:]
        total = each[:, :LANES]
        for d in range(1, DETS):
            total = total + each[:, d * LANES : (d + 1) * LANES]
        return total

    @pl.when(rate == 0)
    def _():
        for c in range(OUT0 // LANES):
            out_ref[0, :, c * LANES : (c + 1) * LANES] = power(c)

    @pl.when(rate > 0)
    def _():
        total = jnp.concatenate([power(0), power(1)], axis=1)
        high = total.astype(BF16)
        rest = total - high.astype(F32)
        middle = rest.astype(BF16)
        low = (rest - middle.astype(F32)).astype(BF16)
        shape = (2 * LANES, OUT0)
        spread = (iota(shape, 1) >> rate) == iota(shape, 0)
        spread = spread.astype(F32).astype(BF16)
        out = jnp.dot(high, spread, preferred_element_type=F32)
        out = out + jnp.dot(middle, spread, preferred_element_type=F32)
        out_ref[0] = out + jnp.dot(low, spread, preferred_element_type=F32)


def on_device(strain, filters, mixing, counts, rate_bands):
    smem = pl.BlockSpec(memory_space=pltpu.SMEM)
    vmem = pl.BlockSpec(memory_space=pltpu.VMEM)
    anywhere = pl.BlockSpec(memory_space=pl.ANY)
    dma = pltpu.SemaphoreType.DMA
    seen, bank = pl.pallas_call(
        gather_kernel,
        out_shape=(
            jax.ShapeDtypeStruct((NE, NY, 16, LANES), BF16),
            jax.ShapeDtypeStruct((2 * PART, TAPS), BF16),
        ),
        in_specs=[smem, vmem, anywhere, anywhere],
        out_specs=(vmem, vmem),
        scratch_shapes=[
            pltpu.VMEM((1, 3 * LANES), F32),
            pltpu.VMEM((8 * NZ, LANES), F32),
            pltpu.VMEM((1, KMAX, TAPS), BF16),
            pltpu.VMEM((1, 2, PART, KMAX), BF16),
            dma((2,)),
            dma((NZ - 1,)),
            dma((NZ - 1,)),
            dma((NY - 1,)),
            dma((NY - 1,)),
            dma((NE - 1,)),
            dma((NE - 1,)),
        ],
        compiler_params=pltpu.CompilerParams(
            collective_id=0, has_side_effects=True, vmem_limit_bytes=24 * 2**20
        ),
        name="gather_and_mix",
    )(counts, strain, filters, mixing)
    return pl.pallas_call(
        filter_kernel,
        out_shape=jax.ShapeDtypeStruct((1, PART, OUT0), F32),
        in_specs=[smem, vmem, vmem],
        out_specs=vmem,
        scratch_shapes=[
            pltpu.VMEM((16, DETS * LANES), F32),
            pltpu.VMEM((11 * LANES, DETS * LANES), BF16),
        ],
        compiler_params=pltpu.CompilerParams(vmem_limit_bytes=24 * 2**20),
        name="filter_and_sum",
    )(rate_bands, seen, bank)


def solution(mesh):
    placed = (
        P("det", "bins"),
        P("bins", None, None),
        P("bins", None, None, None),
        P("bins"),
        P("bins"),
    )
    return jax.shard_map(
        on_device, mesh=mesh, in_specs=placed, out_specs=P("bins", "det", None), check_vma=False
    )
```

```python
import jax
import jax.numpy as jnp
from jax import lax
from jax.experimental import pallas as pl
from jax.experimental.pallas import tpu as pltpu
from jax.sharding import PartitionSpec as P

DETS = 4
KMAX = 512
TAPS = 1024
TPL = 256
OUT0 = 512
SAMPLES = 17408
SHARD = 272
NZ, NY, NX = 8, 4, 2
PART = TPL // DETS
LANES = 128
MESH = pl.DeviceIdType.MESH
F32 = jnp.float32
BF16 = jnp.bfloat16
WIDTH = (272, 136, 68, 34, 17)
COLUMN = (0, 0, 136, 204, 238)
START = tuple((SAMPLES >> r) - (OUT0 >> r) - (TAPS - 1) for r in range(5))


def iota(shape, dim):
    return lax.broadcasted_iota(jnp.int32, shape, dim)


def ladder_matrix():
    col = iota((1, 2 * LANES), 1)
    sample = iota((3 * LANES, 2 * LANES), 0)
    matrix = jnp.zeros((3 * LANES, 2 * LANES), F32)
    for r in range(1, 5):
        here = (col >= COLUMN[r]) & (col < COLUMN[r] + WIDTH[r])
        matrix = jnp.where(here & ((sample >> r) == col - COLUMN[r]), 0.5**r, matrix)
    return matrix.astype(BF16)


def hops(step, n):
    return min(step, n - step)


def gather_kernel(
    counts_hbm,
    rates_hbm,
    strain_hbm,
    filters_hbm,
    mixing_hbm,
    seen_ref,
    bank_ref,
    rates_ref,
    counts,
    rates,
    strain,
    padded,
    column,
    filters,
    mixing,
    local_sem,
    line_send,
    line_recv,
    plane_send,
    plane_recv,
):
    at_bin = lax.axis_index("bins")
    det = lax.axis_index("det")
    z = at_bin // (NY * NX)
    y = (at_bin // NX) % NY
    x = (at_bin % NX) * 2 + det // 2
    core = det % 2

    def device(z, y, x, core):
        return (z * NY + y) * NX + x // 2, (x % 2) * 2 + core

    line = [(dz, dc) for dz in range(NZ) for dc in range(2)][1:]
    line.sort(key=lambda step: -hops(step[0], NZ))
    plane = [(dy, dx) for dy in range(NY) for dx in range(4)][1:]
    plane.sort(key=lambda step: -hops(step[0], NY) - hops(step[1], 4))
    line_peers = [device((z + dz) % NZ, y, x, (core + dc) % 2) for dz, dc in line]
    plane_peers = [device(z, (y + dy) % NY, (x + dx) % 4, core) for dy, dx in plane]

    load_strain = pltpu.make_async_copy(strain_hbm, strain, local_sem.at[0])
    load_strain.start()
    barrier = pltpu.get_barrier_semaphore()
    for peer in line_peers + plane_peers:
        pl.semaphore_signal(barrier, inc=1, device_id=peer, device_id_type=MESH)

    rows = pl.ds(pl.multiple_of(det * PART, PART), PART)
    loads = [
        pltpu.make_async_copy(counts_hbm, counts, local_sem.at[1]),
        pltpu.make_async_copy(rates_hbm, rates, local_sem.at[2]),
        pltpu.make_async_copy(mixing_hbm.at[:, :, rows, :], mixing, local_sem.at[3]),
        pltpu.make_async_copy(filters_hbm, filters, local_sem.at[4]),
    ]
    for load in loads:
        load.start()

    padded[...] = jnp.zeros_like(padded)
    matrix = ladder_matrix()
    load_strain.wait()
    padded[:, 0:SHARD] = strain[...]
    samples = padded[...]
    high = samples.astype(BF16).astype(F32)
    middle = (samples - high).astype(BF16).astype(F32)
    low = samples - high - middle
    part = iota((8, 3 * LANES), 0)
    wide = [jnp.broadcast_to(p, (8, 3 * LANES)) for p in (high, middle, low)]
    parts = jnp.where(
        part == 0, wide[0], jnp.where(part == 1, wide[1], jnp.where(part == 2, wide[2], 0.0))
    )
    split = jnp.dot(parts.astype(BF16), matrix, preferred_element_type=F32)
    ladder = jnp.sum(split, axis=0, keepdims=True)
    row = iota((8, LANES), 0)
    tile = jnp.zeros((8, LANES), F32)
    lines = [ladder[:, :LANES], ladder[:, LANES:]]
    lines += [samples[:, k * LANES : (k + 1) * LANES] for k in range(3)]
    for k, one in enumerate(lines):
        tile = jnp.where(row == k, jnp.broadcast_to(one, (8, LANES)), tile)
    own = pl.ds(pl.multiple_of((core * NZ + z) * 8, 8), 8)
    column[own, :] = tile

    pl.semaphore_wait(barrier, len(line_peers) + len(plane_peers))

    def send(ref, send_sem, recv_sem, peer):
        copy = pltpu.make_async_remote_copy(
            src_ref=ref,
            dst_ref=ref,
            send_sem=send_sem,
            recv_sem=recv_sem,
            device_id=peer,
            device_id_type=MESH,
        )
        copy.start()
        return copy

    line_copies = [
        send(column.at[own, :], line_send.at[k], line_recv.at[k], peer)
        for k, peer in enumerate(line_peers)
    ]

    for load in loads:
        load.wait()
    rates_ref[...] = jnp.full((8, LANES), rates[0, 0], jnp.int32)
    live = iota((1, KMAX), 1) < counts[0, 0]
    mixed = mixing[...].reshape(2 * PART, KMAX)
    mixed = jnp.where(live, mixed, jnp.zeros_like(mixed))
    bank = jnp.dot(mixed, filters[0], preferred_element_type=F32).astype(BF16)
    square = (LANES, LANES)
    turn = (iota(square, 0) + iota(square, 1) == LANES - 1).astype(F32).astype(BF16)
    for a in range(TAPS // LANES):
        taps = slice(a * LANES, (a + 1) * LANES)
        bank_ref[:, taps] = jnp.dot(bank[:, taps], turn, preferred_element_type=F32).astype(BF16)

    for copy in line_copies:
        copy.wait_recv()
    place = y * 4 + x
    for c in range(2):
        first = c * NZ * 8
        low_rows = column[pl.ds(first + 1, 8, stride=8), :]
        last = column[first + 56 : first + 64, :]
        before = column[first + 48 : first + 56, :]
        high_rows = jnp.where(row == 5, jnp.broadcast_to(before[0:1], (8, LANES)), last)
        seen_ref[place, c] = jnp.concatenate([low_rows, high_rows], axis=0).astype(BF16)

    plane_copies = [
        send(seen_ref.at[place], plane_send.at[k], plane_recv.at[k], peer)
        for k, peer in enumerate(plane_peers)
    ]
    for copy in line_copies:
        copy.wait_send()
    for copy in plane_copies:
        copy.wait_recv()
    for copy in plane_copies:
        copy.wait_send()


def flatten(r, seen_ref, flat):
    lane = iota((8, LANES), 1)
    row = iota((8, LANES), 0)
    halves = {4: "low", 3: "low", 2: "low", 1: "both", 0: "high"}[r]
    width = WIDTH[r]
    picks = []
    moved = [[] for _ in range(DETS)]
    out_row16 = iota((16, 8), 0)
    for y in range(NY):
        for xh in range(NX):
            j = y * NX + xh
            jobs = []
            if halves == "low":
                first = COLUMN[r] - LANES
                jobs.append((0, [8 * z + j for z in range(8)], 0, first, [width] * 8))
            if halves == "both":
                jobs.append((0, [8 * z + j for z in range(8)], LANES, 0, [8] * 8))
                jobs.append(
                    (1, [8 * 7 + j, 0, 0, 0, 0, 8 * 6 + j, 0, 0], 0, 0, [LANES, 0, 0, 0, 0, LANES, 0, 0])
                )
            if halves == "high":
                jobs.append((1, [8 * 7 + j] * 8, None, 0, [0, 0, LANES, LANES, 16, 0, 0, 0]))
            for half, shards, skip, first, widths in jobs:
                begin, shift = [], []
                for k in range(8):
                    extra = (k - 2) * LANES if skip is None else skip
                    at = width * shards[k] + extra - START[r]
                    begin.append(at)
                    shift.append((at - first) % LANES)
                stride = (shift[1] - shift[0]) % LANES
                if any((shift[k] - shift[0] - k * stride) % LANES for k in range(8)):
                    stride = None
                begin_row = jnp.zeros((8, LANES), jnp.int32)
                begin_col = jnp.zeros((16, 8), jnp.int32)
                wide = jnp.zeros((8, LANES), jnp.int32)
                for k in range(8):
                    begin_row = jnp.where(row == k, begin[k], begin_row)
                    begin_col = jnp.where(iota((16, 8), 1) == k, begin[k], begin_col)
                    wide = jnp.where(row == k, widths[k], wide)
                offset = (lane - begin_row) & (LANES - 1)
                wraps = ((begin_row & (LANES - 1)) + offset) >= LANES
                for wrap in (False, True):
                    picks.append((begin_col >> 7) + int(wrap) == out_row16)
                for d in range(DETS):
                    block = seen_ref[y * 4 + xh * 2 + d // 2, d % 2].astype(F32)[8 * half : 8 * half + 8]
                    if stride is None:
                        turned = jnp.zeros((8, LANES), F32)
                        for amount in sorted(set(s for s, w in zip(shift, widths) if w)):
                            rolled = pltpu.roll(block, amount, 1)
                            mask = jnp.zeros((8, LANES), jnp.bool_)
                            for k in range(8):
                                if shift[k] == amount:
                                    mask = mask | (row == k)
                            turned = jnp.where(mask, rolled, turned)
                    elif stride == 0:
                        turned = pltpu.roll(block, shift[0], 1)
                    else:
                        turned = pltpu.roll(block, shift[0], 1)
                        step = min(stride, 16)
                        for _ in range(stride // step):
                            turned = pltpu.roll(turned, 0, 1, stride=step, stride_axis=0)
                    for wrap in (False, True):
                        keep = (offset < wide) & (wraps == wrap)
                        moved[d].append(jnp.where(keep, turned, 0.0))
    pick = jnp.concatenate([p.astype(F32) for p in picks], axis=1).astype(BF16)
    for d in range(DETS):
        data = jnp.concatenate(moved[d], axis=0).astype(BF16)
        flat[:, d * LANES : (d + 1) * LANES] = jnp.dot(pick, data, preferred_element_type=F32)


def filter_kernel(rates_ref, seen_ref, bank_ref, out_ref, flat, hankel):
    rate = rates_ref[...][0, 0]
    for r in range(5):

        @pl.when(rate == r)
        def _(r=r):
            flatten(r, seen_ref, flat)

    square = (LANES, LANES)
    later = iota(square, 1) > iota(square, 0)
    blocks = OUT0 // LANES + TAPS // LANES - 1
    for d in range(DETS):
        cols = slice(d * LANES, (d + 1) * LANES)
        turned = None
        for m in range(blocks + 1):
            line = jnp.broadcast_to(flat[m : m + 1, cols], square)
            following = pltpu.roll(line, 1, 1, stride=1, stride_axis=0)
            if m:
                hankel[(m - 1) * LANES : m * LANES, cols] = jnp.where(
                    later, following, turned
                ).astype(BF16)
            turned = following

    def power(c):
        snr = jnp.dot(
            bank_ref[...], hankel[c * LANES : c * LANES + TAPS, :], preferred_element_type=F32
        )
        each = snr[:PART] * snr[:PART] + snr[PART:] * snr[PART:]
        total = each[:, :LANES]
        for d in range(1, DETS):
            total = total + each[:, d * LANES : (d + 1) * LANES]
        return total

    @pl.when(rate == 0)
    def _():
        for c in range(OUT0 // LANES):
            out_ref[0, :, c * LANES : (c + 1) * LANES] = power(c)

    @pl.when(rate > 0)
    def _():
        total = jnp.concatenate([power(0), power(1)], axis=1)
        high = total.astype(BF16)
        rest = total - high.astype(F32)
        middle = rest.astype(BF16)
        low = (rest - middle.astype(F32)).astype(BF16)
        shape = (2 * LANES, OUT0)
        spread = (iota(shape, 1) >> rate) == iota(shape, 0)
        spread = spread.astype(F32).astype(BF16)
        out = jnp.dot(high, spread, preferred_element_type=F32)
        out = out + jnp.dot(middle, spread, preferred_element_type=F32)
        out_ref[0] = out + jnp.dot(low, spread, preferred_element_type=F32)


def on_device(strain, filters, mixing, counts, rate_bands):
    vmem = pl.BlockSpec(memory_space=pltpu.VMEM)
    hbm = pl.BlockSpec(memory_space=pltpu.HBM)
    dma = pltpu.SemaphoreType.DMA
    given = (counts.reshape(1, 1), rate_bands.reshape(1, 1), strain, filters, mixing)
    given = given[:2] + tuple(pltpu.with_memory_space_constraint(one, pltpu.HBM) for one in given[2:])
    seen, bank, rates = pl.pallas_call(
        gather_kernel,
        out_shape=(
            jax.ShapeDtypeStruct((NY * 4, 2, 16, LANES), BF16),
            jax.ShapeDtypeStruct((2 * PART, TAPS), BF16),
            jax.ShapeDtypeStruct((8, LANES), jnp.int32),
        ),
        in_specs=[hbm] * 5,
        out_specs=(vmem, vmem, vmem),
        scratch_shapes=[
            pltpu.SMEM((1, 1), jnp.int32),
            pltpu.SMEM((1, 1), jnp.int32),
            pltpu.VMEM((1, SHARD), F32),
            pltpu.VMEM((1, 3 * LANES), F32),
            pltpu.VMEM((2 * NZ * 8, LANES), F32),
            pltpu.VMEM((1, KMAX, TAPS), BF16),
            pltpu.VMEM((1, 2, PART, KMAX), BF16),
            dma((5,)),
            dma((2 * NZ - 1,)),
            dma((2 * NZ - 1,)),
            dma((NY * 4 - 1,)),
            dma((NY * 4 - 1,)),
        ],
        compiler_params=pltpu.CompilerParams(
            collective_id=0, has_side_effects=True, vmem_limit_bytes=24 * 2**20
        ),
        name="gather_and_mix",
    )(*given)
    return pl.pallas_call(
        filter_kernel,
        out_shape=jax.ShapeDtypeStruct((1, PART, OUT0), F32),
        in_specs=[vmem, vmem, vmem],
        out_specs=vmem,
        scratch_shapes=[
            pltpu.VMEM((16, DETS * LANES), F32),
            pltpu.VMEM((11 * LANES, DETS * LANES), BF16),
        ],
        compiler_params=pltpu.CompilerParams(vmem_limit_bytes=24 * 2**20),
        name="filter_and_sum",
    )(rates, seen, bank)


def solution(mesh):
    placed = (
        P("det", "bins"),
        P("bins", None, None),
        P("bins", None, None, None),
        P("bins"),
        P("bins"),
    )
    return jax.shard_map(
        on_device, mesh=mesh, in_specs=placed, out_specs=P("bins", "det", None), check_vma=False
    )
```

```python
import jax
import jax.numpy as jnp
from jax import lax
from jax.experimental import pallas as pl
from jax.experimental.pallas import tpu as pltpu
from jax.sharding import PartitionSpec as P

DETS = 4
KMAX = 512
TAPS = 1024
TPL = 256
OUT0 = 512
SAMPLES = 17408
SHARD = 272
NZ, NY, NX = 8, 4, 2
PART = TPL // DETS
LANES = 128
MESH = pl.DeviceIdType.MESH
F32 = jnp.float32
BF16 = jnp.bfloat16
WIDTH = (272, 136, 68, 34, 17)
COLUMN = (0, 0, 136, 204, 238)
START = tuple((SAMPLES >> r) - (OUT0 >> r) - (TAPS - 1) for r in range(5))


LINES = (
    (4, 1, 110, 0, 17),
    (3, 1, 76, 0, 34),
    (2, 1, 8, 0, 68),
    (1, 0, 0, 0, 128),
    (1, 1, 0, 128, 8),
    (0, 2, 0, 0, 128),
    (0, 3, 0, 128, 128),
    (0, 4, 0, 256, 16),
)
ROWS = ((5, 7), (0, 3), (2, 4), (4, 7), (0, 7))


def iota(shape, dim):
    return lax.broadcasted_iota(jnp.int32, shape, dim)


def ladder_matrix():
    col = iota((1, 2 * LANES), 1)
    sample = iota((3 * LANES, 2 * LANES), 0)
    matrix = jnp.zeros((3 * LANES, 2 * LANES), F32)
    for r in range(1, 5):
        here = (col >= COLUMN[r]) & (col < COLUMN[r] + WIDTH[r])
        matrix = jnp.where(here & ((sample >> r) == col - COLUMN[r]), 0.5**r, matrix)
    return matrix.astype(BF16)


def hops(step, n):
    return min(step, n - step)


def gather_kernel(
    counts_hbm,
    rates_hbm,
    strain_hbm,
    filters_hbm,
    mixing_hbm,
    seen_ref,
    bank_ref,
    rates_ref,
    counts,
    rates,
    strain,
    padded,
    column,
    filters,
    mixing,
    local_sem,
    line_send,
    line_recv,
    plane_send,
    plane_recv,
):
    at_bin = lax.axis_index("bins")
    det = lax.axis_index("det")
    z = at_bin // (NY * NX)
    y = (at_bin // NX) % NY
    x = (at_bin % NX) * 2 + det // 2
    core = det % 2

    def device(z, y, x, core):
        return (z * NY + y) * NX + x // 2, (x % 2) * 2 + core

    line = [(dz, dc) for dz in range(NZ) for dc in range(2)][1:]
    line.sort(key=lambda step: -hops(step[0], NZ))
    plane = [(dy, dx) for dy in range(NY) for dx in range(4)][1:]
    plane.sort(key=lambda step: -hops(step[0], NY) - hops(step[1], 4))
    line_peers = [device((z + dz) % NZ, y, x, (core + dc) % 2) for dz, dc in line]
    plane_peers = [device(z, (y + dy) % NY, (x + dx) % 4, core) for dy, dx in plane]

    load_strain = pltpu.make_async_copy(strain_hbm, strain, local_sem.at[0])
    load_strain.start()
    barrier = pltpu.get_barrier_semaphore()
    for peer in line_peers + plane_peers:
        pl.semaphore_signal(barrier, inc=1, device_id=peer, device_id_type=MESH)

    rows = pl.ds(pl.multiple_of(det * PART, PART), PART)
    loads = [
        pltpu.make_async_copy(counts_hbm, counts, local_sem.at[1]),
        pltpu.make_async_copy(rates_hbm, rates, local_sem.at[2]),
        pltpu.make_async_copy(mixing_hbm.at[:, :, rows, :], mixing, local_sem.at[3]),
        pltpu.make_async_copy(filters_hbm, filters, local_sem.at[4]),
    ]
    for load in loads:
        load.start()

    padded[...] = jnp.zeros_like(padded)
    matrix = ladder_matrix()
    load_strain.wait()
    padded[:, 0:SHARD] = strain[...]
    samples = padded[...]
    high = samples.astype(BF16).astype(F32)
    middle = (samples - high).astype(BF16).astype(F32)
    low = samples - high - middle
    part = iota((8, 3 * LANES), 0)
    wide = [jnp.broadcast_to(p, (8, 3 * LANES)) for p in (high, middle, low)]
    parts = jnp.where(
        part == 0, wide[0], jnp.where(part == 1, wide[1], jnp.where(part == 2, wide[2], 0.0))
    )
    split = jnp.dot(parts.astype(BF16), matrix, preferred_element_type=F32)
    ladder = jnp.sum(split, axis=0, keepdims=True)
    row = iota((8, LANES), 0)
    lane = iota((8, LANES), 1)
    halves = [ladder[:, :LANES], ladder[:, LANES:]]
    halves += [samples[:, k * LANES : (k + 1) * LANES] for k in range(3)]
    tile = jnp.zeros((8, LANES), F32)
    for k, (r, half, first, skip, width) in enumerate(LINES):
        line = jnp.broadcast_to(halves[half], (8, LANES))
        line = jnp.where((lane >= first) & (lane < first + width), line, 0.0)
        turn = (WIDTH[r] * at_bin + skip + (LANES * 256 - START[r] - first)) % LANES
        tile = jnp.where(row == k, pltpu.roll(line, turn, 1), tile)
    own = pl.ds(pl.multiple_of((core * NZ + z) * 8, 8), 8)
    column[own, :] = tile

    pl.semaphore_wait(barrier, len(line_peers) + len(plane_peers))

    def send(ref, send_sem, recv_sem, peer):
        copy = pltpu.make_async_remote_copy(
            src_ref=ref,
            dst_ref=ref,
            send_sem=send_sem,
            recv_sem=recv_sem,
            device_id=peer,
            device_id_type=MESH,
        )
        copy.start()
        return copy

    line_copies = [
        send(column.at[own, :], line_send.at[k], line_recv.at[k], peer)
        for k, peer in enumerate(line_peers)
    ]

    for load in loads:
        load.wait()
    rates_ref[...] = jnp.full((8, LANES), rates[0, 0], jnp.int32)
    live = iota((1, KMAX), 1) < counts[0, 0]
    mixed = mixing[...].reshape(2 * PART, KMAX)
    mixed = jnp.where(live, mixed, jnp.zeros_like(mixed))
    bank = jnp.dot(mixed, filters[0], preferred_element_type=F32).astype(BF16)
    square = (LANES, LANES)
    turn = (iota(square, 0) + iota(square, 1) == LANES - 1).astype(F32).astype(BF16)
    for a in range(TAPS // LANES):
        taps = slice(a * LANES, (a + 1) * LANES)
        bank_ref[:, taps] = jnp.dot(bank[:, taps], turn, preferred_element_type=F32).astype(BF16)

    for copy in line_copies:
        copy.wait_recv()
    place = y * 4 + x
    for c in range(2):
        first = c * NZ * 8
        lines = [column[pl.ds(first + k, 8, stride=8), :] for k in range(5)]
        last = column[first + 56 : first + 64, :]
        low = lines[0] + pltpu.roll(lines[0], 5, 0)
        low = low + jnp.where(row < 2, pltpu.roll(lines[0], 2, 0), 0.0)
        tail = pltpu.roll(lines[4], 5, 0) + pltpu.roll(lines[4], 4, 0)
        top = jnp.where(row < 3, low, jnp.where(row < 4, tail, lines[1]))
        bottom = jnp.where(row < 2, pltpu.roll(lines[3], 2, 0), pltpu.roll(lines[2], 5, 0))
        bottom = jnp.where(row < 5, bottom, last)
        packed = jnp.concatenate([top, bottom], axis=0)
        seen_ref[place, c] = packed.astype(BF16)

    plane_copies = [
        send(seen_ref.at[place], plane_send.at[k], plane_recv.at[k], peer)
        for k, peer in enumerate(plane_peers)
    ]
    for copy in line_copies:
        copy.wait_send()
    for copy in plane_copies:
        copy.wait_recv()
    for copy in plane_copies:
        copy.wait_send()


def begins(r, k, j):
    at, extra = k, 0
    if r == 2:
        at = k + 3
    if r == 1:
        at, extra = (k & 1) + 6, LANES * (k >> 1)
    if r == 0:
        at, extra = 7, LANES * (k - 5)
    return WIDTH[r] * (8 * at + j) + extra - START[r]


def flatten(r, seen_ref, flat):
    least, most = ROWS[r]
    row = iota((8, LANES), 0)
    lane = iota((8, LANES), 1)
    moved = [[] for _ in range(DETS)]
    for y in range(NY):
        for xh in range(NX):
            begin = begins(r, row, y * NX + xh) & (LANES - 1)
            after = lane >= begin
            before = lane < begin
            if r == 4 or r == 1:
                inside = ((lane - begin) & (LANES - 1)) < (WIDTH[4] if r == 4 else 8)
                if r == 1:
                    inside = inside | (row < 2)
                after, before = after & inside, before & inside
            for d in range(DETS):
                pair = seen_ref[y * 4 + xh * 2 + d // 2, d % 2].astype(F32)
                top, bottom = pair[:8], pair[8:]
                if r == 4:
                    block = jnp.where(row < 6, pltpu.roll(top, 3, 0), pltpu.roll(top, 6, 0))
                    block = jnp.where(row < 3, top, block)
                elif r == 1:
                    block = jnp.where(row < 2, bottom, jnp.broadcast_to(top[3:4], (8, LANES)))
                else:
                    block = top if r == 3 else bottom
                moved[d].append(jnp.where(after, block, 0.0))
                moved[d].append(jnp.where(before, block, 0.0))
    shape = (16, 2 * 8 * NY * NX)
    at = iota(shape, 1)
    k = at & 7
    where = (begins(r, k, at >> 4) >> 7) + ((at >> 3) & 1)
    pick = (where == iota(shape, 0)) & (k >= least) & (k <= most)
    data = jnp.concatenate([jnp.concatenate(m, axis=0) for m in moved], axis=1).astype(BF16)
    flat[...] = jnp.dot(pick.astype(F32).astype(BF16), data, preferred_element_type=F32)


def build_hankel(flat, hankel, blocks, first=0):
    square = (LANES, LANES)
    later = iota(square, 1) > iota(square, 0)

    for d in range(DETS):
        cols = slice(d * LANES, (d + 1) * LANES)
        turned = None
        for m in range(first, blocks + 1):
            line = jnp.broadcast_to(flat[m : m + 1, cols], square)
            following = pltpu.roll(line, 1, 1, stride=1, stride_axis=0)
            if m > first:
                hankel[(m - 1) * LANES : m * LANES, cols] = jnp.where(
                    later, following, turned
                ).astype(BF16)
            turned = following


def filter_kernel(rates_ref, seen_ref, bank_ref, out_ref, flat, hankel):
    rate = rates_ref[...][0, 0]
    def total_of(snr):
        each = snr[:PART] * snr[:PART] + snr[PART:] * snr[PART:]
        total = each[:, :LANES]
        for d in range(1, DETS):
            total = total + each[:, d * LANES : (d + 1) * LANES]
        return total

    def power(c):
        taps = hankel[c * LANES : c * LANES + TAPS, :]
        return total_of(jnp.dot(bank_ref[...], taps, preferred_element_type=F32))

    def repeat(total):
        high = total.astype(BF16)
        rest = total - high.astype(F32)
        middle = rest.astype(BF16)
        low = (rest - middle.astype(F32)).astype(BF16)
        shape = (total.shape[1], OUT0)
        spread = (iota(shape, 1) >> rate) == iota(shape, 0)
        spread = spread.astype(F32).astype(BF16)
        out = jnp.dot(high, spread, preferred_element_type=F32)
        out = out + jnp.dot(middle, spread, preferred_element_type=F32)
        out_ref[0] = out + jnp.dot(low, spread, preferred_element_type=F32)

    blocks = TAPS // LANES

    @pl.when(rate == 0)
    def _():
        flatten(0, seen_ref, flat)
        build_hankel(flat, hankel, blocks + 3)
        for c in range(OUT0 // LANES):
            out_ref[0, :, c * LANES : (c + 1) * LANES] = power(c)

    @pl.when(rate == 1)
    def _():
        flatten(1, seen_ref, flat)
        build_hankel(flat, hankel, blocks + 1)
        repeat(jnp.concatenate([power(0), power(1)], axis=1))

    for r in range(2, 5):

        @pl.when(rate == r)
        def _(r=r):
            flatten(r, seen_ref, flat)

    @pl.when(rate > 1)
    def _():
        build_hankel(flat, hankel, blocks)
        repeat(power(0))


def on_device(strain, filters, mixing, counts, rate_bands):
    vmem = pl.BlockSpec(memory_space=pltpu.VMEM)
    hbm = pl.BlockSpec(memory_space=pltpu.HBM)
    dma = pltpu.SemaphoreType.DMA
    given = (counts.reshape(1, 1), rate_bands.reshape(1, 1), strain, filters, mixing)
    given = given[:2] + tuple(pltpu.with_memory_space_constraint(one, pltpu.HBM) for one in given[2:])
    seen, bank, rates = pl.pallas_call(
        gather_kernel,
        out_shape=(
            jax.ShapeDtypeStruct((NY * 4, 2, 16, LANES), BF16),
            jax.ShapeDtypeStruct((2 * PART, TAPS), BF16),
            jax.ShapeDtypeStruct((8, LANES), jnp.int32),
        ),
        in_specs=[hbm] * 5,
        out_specs=(vmem, vmem, vmem),
        scratch_shapes=[
            pltpu.SMEM((1, 1), jnp.int32),
            pltpu.SMEM((1, 1), jnp.int32),
            pltpu.VMEM((1, SHARD), F32),
            pltpu.VMEM((1, 3 * LANES), F32),
            pltpu.VMEM((2 * NZ * 8, LANES), F32),
            pltpu.VMEM((1, KMAX, TAPS), BF16),
            pltpu.VMEM((1, 2, PART, KMAX), BF16),
            dma((5,)),
            dma((2 * NZ - 1,)),
            dma((2 * NZ - 1,)),
            dma((NY * 4 - 1,)),
            dma((NY * 4 - 1,)),
        ],
        compiler_params=pltpu.CompilerParams(
            collective_id=0, has_side_effects=True, vmem_limit_bytes=24 * 2**20
        ),
        name="gather_and_mix",
    )(*given)
    return pl.pallas_call(
        filter_kernel,
        out_shape=jax.ShapeDtypeStruct((1, PART, OUT0), F32),
        in_specs=[vmem, vmem, vmem],
        out_specs=vmem,
        scratch_shapes=[
            pltpu.VMEM((16, DETS * LANES), F32),
            pltpu.VMEM((11 * LANES, DETS * LANES), BF16),
        ],
        compiler_params=pltpu.CompilerParams(vmem_limit_bytes=24 * 2**20),
        name="filter_and_sum",
    )(rates, seen, bank)


def solution(mesh):
    placed = (
        P("det", "bins"),
        P("bins", None, None),
        P("bins", None, None, None),
        P("bins"),
        P("bins"),
    )
    return jax.shard_map(
        on_device, mesh=mesh, in_specs=placed, out_specs=P("bins", "det", None), check_vma=False
    )
```

```python
import jax
import jax.numpy as jnp
from jax import lax
from jax.experimental import pallas as pl
from jax.experimental.pallas import tpu as pltpu
from jax.sharding import PartitionSpec as P

DETS = 4
KMAX = 512
TAPS = 1024
TPL = 256
OUT0 = 512
SAMPLES = 17408
SHARD = 272
NZ, NY, NX = 8, 4, 2
PART = TPL // DETS
LANES = 128
MESH = pl.DeviceIdType.MESH
F32 = jnp.float32
BF16 = jnp.bfloat16
WIDTH = (272, 136, 68, 34, 17)
COLUMN = (0, 0, 136, 204, 238)
START = tuple((SAMPLES >> r) - (OUT0 >> r) - (TAPS - 1) for r in range(5))


LINES = (
    (4, 1, 110, 0, 17),
    (3, 1, 76, 0, 34),
    (2, 1, 8, 0, 68),
    (1, 0, 0, 0, 128),
    (1, 1, 0, 128, 8),
    (0, 2, 0, 0, 128),
    (0, 3, 0, 128, 128),
    (0, 4, 0, 256, 16),
)
ROWS = ((5, 7), (0, 3), (2, 4), (4, 7), (0, 7))


def iota(shape, dim):
    return lax.broadcasted_iota(jnp.int32, shape, dim)


def ladder_matrix():
    col = iota((1, 2 * LANES), 1)
    sample = iota((3 * LANES, 2 * LANES), 0)
    matrix = jnp.zeros((3 * LANES, 2 * LANES), F32)
    for r in range(1, 5):
        here = (col >= COLUMN[r]) & (col < COLUMN[r] + WIDTH[r])
        matrix = jnp.where(here & ((sample >> r) == col - COLUMN[r]), 0.5**r, matrix)
    return matrix.astype(BF16)


def hops(step, n):
    return min(step, n - step)


def gather_kernel(
    counts_hbm,
    rates_hbm,
    strain_hbm,
    filters_hbm,
    mixing_hbm,
    seen_ref,
    bank_ref,
    rates_ref,
    counts,
    rates,
    strain,
    padded,
    column,
    filters,
    mixing,
    local_sem,
    line_send,
    line_recv,
    plane_send,
    plane_recv,
):
    at_bin = lax.axis_index("bins")
    det = lax.axis_index("det")
    z = at_bin // (NY * NX)
    y = (at_bin // NX) % NY
    x = (at_bin % NX) * 2 + det // 2
    core = det % 2

    def device(z, y, x, core):
        return (z * NY + y) * NX + x // 2, (x % 2) * 2 + core

    line = [(dz, dc) for dz in range(NZ) for dc in range(2)][1:]
    line.sort(key=lambda step: -hops(step[0], NZ))
    plane = [(dy, dx) for dy in range(NY) for dx in range(4)][1:]
    plane.sort(key=lambda step: -hops(step[0], NY) - hops(step[1], 4))
    line_peers = [device((z + dz) % NZ, y, x, (core + dc) % 2) for dz, dc in line]
    plane_peers = [device(z, (y + dy) % NY, (x + dx) % 4, core) for dy, dx in plane]

    load_strain = pltpu.make_async_copy(strain_hbm, strain, local_sem.at[0])
    load_strain.start()
    barrier = pltpu.get_barrier_semaphore()
    for peer in line_peers + plane_peers:
        pl.semaphore_signal(barrier, inc=1, device_id=peer, device_id_type=MESH)

    rows = pl.ds(pl.multiple_of(det * PART, PART), PART)
    loads = [
        pltpu.make_async_copy(counts_hbm, counts, local_sem.at[1]),
        pltpu.make_async_copy(rates_hbm, rates, local_sem.at[2]),
        pltpu.make_async_copy(mixing_hbm.at[:, :, rows, :], mixing, local_sem.at[3]),
        pltpu.make_async_copy(filters_hbm, filters, local_sem.at[4]),
    ]
    for load in loads:
        load.start()

    padded[...] = jnp.zeros_like(padded)
    matrix = ladder_matrix()
    load_strain.wait()
    padded[:, 0:SHARD] = strain[...]
    samples = padded[...]
    high = samples.astype(BF16).astype(F32)
    middle = (samples - high).astype(BF16).astype(F32)
    low = samples - high - middle
    part = iota((8, 3 * LANES), 0)
    wide = [jnp.broadcast_to(p, (8, 3 * LANES)) for p in (high, middle, low)]
    parts = jnp.where(
        part == 0, wide[0], jnp.where(part == 1, wide[1], jnp.where(part == 2, wide[2], 0.0))
    )
    split = jnp.dot(parts.astype(BF16), matrix, preferred_element_type=F32)
    ladder = jnp.sum(split, axis=0, keepdims=True)
    row = iota((8, LANES), 0)
    lane = iota((8, LANES), 1)
    halves = [ladder[:, :LANES], ladder[:, LANES:]]
    halves += [samples[:, k * LANES : (k + 1) * LANES] for k in range(3)]
    tile = jnp.zeros((8, LANES), F32)
    for k, (r, half, first, skip, width) in enumerate(LINES):
        line = jnp.broadcast_to(halves[half], (8, LANES))
        line = jnp.where((lane >= first) & (lane < first + width), line, 0.0)
        turn = (WIDTH[r] * at_bin + skip + (LANES * 256 - START[r] - first)) % LANES
        tile = jnp.where(row == k, pltpu.roll(line, turn, 1), tile)
    own = pl.ds(pl.multiple_of((core * NZ + z) * 8, 8), 8)
    column[own, :] = tile

    pl.semaphore_wait(barrier, len(line_peers) + len(plane_peers))

    def send(ref, send_sem, recv_sem, peer):
        copy = pltpu.make_async_remote_copy(
            src_ref=ref,
            dst_ref=ref,
            send_sem=send_sem,
            recv_sem=recv_sem,
            device_id=peer,
            device_id_type=MESH,
        )
        copy.start()
        return copy

    line_copies = [
        send(column.at[own, :], line_send.at[k], line_recv.at[k], peer)
        for k, peer in enumerate(line_peers)
    ]

    for load in loads:
        load.wait()
    rates_ref[...] = jnp.full((8, LANES), rates[0, 0], jnp.int32)
    live = iota((1, KMAX), 1) < counts[0, 0]
    mixed = mixing[...].reshape(2 * PART, KMAX)
    mixed = jnp.where(live, mixed, jnp.zeros_like(mixed))
    bank = jnp.dot(mixed, filters[0], preferred_element_type=F32).astype(BF16)
    square = (LANES, LANES)
    turn = (iota(square, 0) + iota(square, 1) == LANES - 1).astype(F32).astype(BF16)
    for a in range(TAPS // LANES):
        taps = slice(a * LANES, (a + 1) * LANES)
        bank_ref[:, taps] = jnp.dot(bank[:, taps], turn, preferred_element_type=F32).astype(BF16)

    for copy in line_copies:
        copy.wait_recv()
    place = y * 4 + x
    for c in range(2):
        first = c * NZ * 8
        lines = [column[pl.ds(first + k, 8, stride=8), :] for k in range(5)]
        last = column[first + 56 : first + 64, :]
        low = lines[0] + pltpu.roll(lines[0], 5, 0)
        low = low + jnp.where(row < 2, pltpu.roll(lines[0], 2, 0), 0.0)
        tail = pltpu.roll(lines[4], 5, 0) + pltpu.roll(lines[4], 4, 0)
        top = jnp.where(row < 3, low, jnp.where(row < 4, tail, lines[1]))
        bottom = jnp.where(row < 2, pltpu.roll(lines[3], 2, 0), pltpu.roll(lines[2], 5, 0))
        bottom = jnp.where(row < 5, bottom, last)
        packed = jnp.concatenate([top, bottom], axis=0)
        seen_ref[place, c] = packed.astype(BF16)

    plane_copies = [
        send(seen_ref.at[place], plane_send.at[k], plane_recv.at[k], peer)
        for k, peer in enumerate(plane_peers)
    ]
    for copy in line_copies:
        copy.wait_send()
    for copy in plane_copies:
        copy.wait_recv()
    for copy in plane_copies:
        copy.wait_send()


def begins(r, k, j):
    at, extra = k, 0
    if r == 2:
        at = k + 3
    if r == 1:
        at, extra = (k & 1) + 6, LANES * (k >> 1)
    if r == 0:
        at, extra = 7, LANES * (k - 5)
    return WIDTH[r] * (8 * at + j) + extra - START[r]


def flatten(r, seen_ref, flat):
    least, most = ROWS[r]
    row = iota((8, LANES), 0)
    lane = iota((8, LANES), 1)
    moved = [[] for _ in range(DETS)]
    for y in range(NY):
        for xh in range(NX):
            begin = begins(r, row, y * NX + xh) & (LANES - 1)
            after = lane >= begin
            before = lane < begin
            if r == 4 or r == 1:
                inside = ((lane - begin) & (LANES - 1)) < (WIDTH[4] if r == 4 else 8)
                if r == 1:
                    inside = inside | (row < 2)
                after, before = after & inside, before & inside
            for d in range(DETS):
                pair = seen_ref[y * 4 + xh * 2 + d // 2, d % 2].astype(F32)
                top, bottom = pair[:8], pair[8:]
                if r == 4:
                    block = jnp.where(row < 6, pltpu.roll(top, 3, 0), pltpu.roll(top, 6, 0))
                    block = jnp.where(row < 3, top, block)
                elif r == 1:
                    block = jnp.where(row < 2, bottom, jnp.broadcast_to(top[3:4], (8, LANES)))
                else:
                    block = top if r == 3 else bottom
                moved[d].append(jnp.where(after, block, 0.0))
                moved[d].append(jnp.where(before, block, 0.0))
    shape = (16, 2 * 8 * NY * NX)
    at = iota(shape, 1)
    k = at & 7
    where = (begins(r, k, at >> 4) >> 7) + ((at >> 3) & 1)
    pick = (where == iota(shape, 0)) & (k >= least) & (k <= most)
    data = jnp.concatenate([jnp.concatenate(m, axis=0) for m in moved], axis=1).astype(BF16)
    flat[...] = jnp.dot(pick.astype(F32).astype(BF16), data, preferred_element_type=F32)


def build_hankel(flat, hankel, blocks):
    rows = 16
    shape = (rows, LANES)
    groups = range(LANES // rows)
    later = [iota(shape, 1) > iota(shape, 0) + rows * g for g in groups]
    for d in range(DETS):
        cols = slice(d * LANES, (d + 1) * LANES)
        turned = None
        for m in range(blocks + 1):
            line = jnp.broadcast_to(flat[m : m + 1, cols], shape)
            line = pltpu.roll(line, 1, 1, stride=1, stride_axis=0).astype(BF16)
            following = [pltpu.roll(line, rows * g, 1) if g else line for g in groups]
            if m:
                for g in groups:
                    at = (m - 1) * LANES + rows * g
                    hankel[at : at + rows, cols] = jnp.where(later[g], following[g], turned[g])
            turned = following


def filter_kernel(rates_ref, seen_ref, bank_ref, out_hbm, flat, hankel, out, sems):
    rate = rates_ref[...][0, 0]
    def total_of(snr):
        each = snr[:PART] * snr[:PART] + snr[PART:] * snr[PART:]
        total = each[:, :LANES]
        for d in range(1, DETS):
            total = total + each[:, d * LANES : (d + 1) * LANES]
        return total

    def copy_of(c):
        cols = slice(c * LANES, (c + 1) * LANES)
        return pltpu.make_async_copy(out.at[c], out_hbm.at[0, :, cols], sems.at[c])

    def write(c, value):
        out[c] = value
        copy_of(c).start()

    def finish():
        for c in range(OUT0 // LANES):
            copy_of(c).wait()

    def power(c):
        taps = hankel[c * LANES : c * LANES + TAPS, :]
        return total_of(jnp.dot(bank_ref[...], taps, preferred_element_type=F32))

    def repeat(total):
        high = total.astype(BF16)
        rest = total - high.astype(F32)
        middle = rest.astype(BF16)
        low = (rest - middle.astype(F32)).astype(BF16)
        shape = (total.shape[1], OUT0)
        spread = (iota(shape, 1) >> rate) == iota(shape, 0)
        spread = spread.astype(F32).astype(BF16)
        parts = jnp.concatenate([high, middle, low], axis=0)
        wide = jnp.dot(parts, spread, preferred_element_type=F32)
        wide = wide[:PART] + wide[PART : 2 * PART] + wide[2 * PART :]
        for c in range(OUT0 // LANES):
            write(c, wide[:, c * LANES : (c + 1) * LANES])
        finish()

    blocks = TAPS // LANES

    @pl.when(rate == 0)
    def _():
        flatten(0, seen_ref, flat)
        build_hankel(flat, hankel, blocks + 3)
        for c in range(OUT0 // LANES):
            write(c, power(c))
        finish()

    @pl.when(rate == 1)
    def _():
        flatten(1, seen_ref, flat)
        build_hankel(flat, hankel, blocks + 1)
        repeat(jnp.concatenate([power(0), power(1)], axis=1))

    for r in range(2, 5):

        @pl.when(rate == r)
        def _(r=r):
            flatten(r, seen_ref, flat)

    @pl.when(rate > 1)
    def _():
        build_hankel(flat, hankel, blocks)
        repeat(power(0))


def on_device(strain, filters, mixing, counts, rate_bands):
    vmem = pl.BlockSpec(memory_space=pltpu.VMEM)
    hbm = pl.BlockSpec(memory_space=pltpu.HBM)
    dma = pltpu.SemaphoreType.DMA
    given = (counts.reshape(1, 1), rate_bands.reshape(1, 1), strain, filters, mixing)
    given = given[:2] + tuple(pltpu.with_memory_space_constraint(one, pltpu.HBM) for one in given[2:])
    seen, bank, rates = pl.pallas_call(
        gather_kernel,
        out_shape=(
            jax.ShapeDtypeStruct((NY * 4, 2, 16, LANES), BF16),
            jax.ShapeDtypeStruct((2 * PART, TAPS), BF16),
            jax.ShapeDtypeStruct((8, LANES), jnp.int32),
        ),
        in_specs=[hbm] * 5,
        out_specs=(vmem, vmem, vmem),
        scratch_shapes=[
            pltpu.SMEM((1, 1), jnp.int32),
            pltpu.SMEM((1, 1), jnp.int32),
            pltpu.VMEM((1, SHARD), F32),
            pltpu.VMEM((1, 3 * LANES), F32),
            pltpu.VMEM((2 * NZ * 8, LANES), F32),
            pltpu.VMEM((1, KMAX, TAPS), BF16),
            pltpu.VMEM((1, 2, PART, KMAX), BF16),
            dma((5,)),
            dma((2 * NZ - 1,)),
            dma((2 * NZ - 1,)),
            dma((NY * 4 - 1,)),
            dma((NY * 4 - 1,)),
        ],
        compiler_params=pltpu.CompilerParams(
            collective_id=0, has_side_effects=True, vmem_limit_bytes=24 * 2**20
        ),
        name="gather_and_mix",
    )(*given)
    return pl.pallas_call(
        filter_kernel,
        out_shape=jax.ShapeDtypeStruct((1, PART, OUT0), F32),
        in_specs=[vmem, vmem, vmem],
        out_specs=hbm,
        scratch_shapes=[
            pltpu.VMEM((16, DETS * LANES), F32),
            pltpu.VMEM((11 * LANES, DETS * LANES), BF16),
            pltpu.VMEM((OUT0 // LANES, PART, LANES), F32),
            dma((OUT0 // LANES,)),
        ],
        compiler_params=pltpu.CompilerParams(vmem_limit_bytes=24 * 2**20),
        name="filter_and_sum",
    )(rates, seen, bank)


def solution(mesh):
    placed = (
        P("det", "bins"),
        P("bins", None, None),
        P("bins", None, None, None),
        P("bins"),
        P("bins"),
    )
    return jax.shard_map(
        on_device, mesh=mesh, in_specs=placed, out_specs=P("bins", "det", None), check_vma=False
    )
```

```python
import jax
import jax.numpy as jnp
from jax import lax
from jax.experimental import pallas as pl
from jax.experimental.pallas import tpu as pltpu
from jax.sharding import PartitionSpec as P

DETS = 4
KMAX = 512
TAPS = 1024
TPL = 256
OUT0 = 512
SAMPLES = 17408
SHARD = 272
NZ, NY, NX = 8, 4, 2
PART = TPL // DETS
LANES = 128
MESH = pl.DeviceIdType.MESH
F32 = jnp.float32
BF16 = jnp.bfloat16
WIDTH = (272, 136, 68, 34, 17)
COLUMN = (0, 0, 136, 204, 238)
START = tuple((SAMPLES >> r) - (OUT0 >> r) - (TAPS - 1) for r in range(5))


LINES = (
    (4, 1, 110, 0, 17),
    (3, 1, 76, 0, 34),
    (2, 1, 8, 0, 68),
    (1, 0, 0, 0, 128),
    (1, 1, 0, 128, 8),
    (0, 2, 0, 0, 128),
    (0, 3, 0, 128, 128),
    (0, 4, 0, 256, 16),
)
ROWS = ((5, 7), (0, 3), (2, 4), (4, 7), (0, 7))


def iota(shape, dim):
    return lax.broadcasted_iota(jnp.int32, shape, dim)


def ladder_matrix():
    col = iota((1, 2 * LANES), 1)
    sample = iota((3 * LANES, 2 * LANES), 0)
    matrix = jnp.zeros((3 * LANES, 2 * LANES), F32)
    for r in range(1, 5):
        here = (col >= COLUMN[r]) & (col < COLUMN[r] + WIDTH[r])
        matrix = jnp.where(here & ((sample >> r) == col - COLUMN[r]), 0.5**r, matrix)
    return matrix.astype(BF16)


def hops(step, n):
    return min(step, n - step)


def mix(sizes_ref, mixing, filters, bank_ref):
    counts = jnp.concatenate([sizes_ref[0:1, :] >> 3] * (KMAX // LANES), axis=1)
    mixed = mixing[...].reshape(2 * PART, KMAX)
    mixed = jnp.where(iota((1, KMAX), 1) < counts, mixed, jnp.zeros_like(mixed))
    bank = jnp.dot(mixed, filters[0], preferred_element_type=F32).astype(BF16)
    square = (LANES, LANES)
    turn = (iota(square, 0) + iota(square, 1) == LANES - 1).astype(F32).astype(BF16)
    for a in range(TAPS // LANES):
        taps = slice(a * LANES, (a + 1) * LANES)
        turned = jnp.dot(bank[:, taps], turn, preferred_element_type=F32)
        bank_ref[: 2 * PART, taps] = turned.astype(BF16)
    rate = (sizes_ref[...] & 7).astype(F32)
    bank_ref[2 * PART :, :LANES] = jnp.concatenate([rate, rate], axis=0).astype(BF16)


def mix_kernel(sizes_ref, filters_hbm, mixing_hbm, bank_ref, filters, mixing, sems):
    rows = pl.ds(pl.multiple_of(lax.axis_index("det") * PART, PART), PART)
    loads = [
        pltpu.make_async_copy(mixing_hbm.at[:, :, rows, :], mixing, sems.at[0]),
        pltpu.make_async_copy(filters_hbm, filters, sems.at[1]),
    ]
    for load in loads:
        load.start()
    for load in loads:
        load.wait()
    mix(sizes_ref, mixing, filters, bank_ref)


def gather_kernel(
    sizes_hbm,
    strain_hbm,
    filters_hbm,
    mixing_hbm,
    seen_ref,
    bank_ref,
    sizes_ref,
    strain,
    padded,
    column,
    filters,
    mixing,
    local_sem,
    line_send,
    line_recv,
    plane_send,
    plane_recv,
):
    at_bin = lax.axis_index("bins")
    det = lax.axis_index("det")
    z = at_bin // (NY * NX)
    y = (at_bin // NX) % NY
    x = (at_bin % NX) * 2 + det // 2
    core = det % 2

    def device(z, y, x, core):
        return (z * NY + y) * NX + x // 2, (x % 2) * 2 + core

    line = [(dz, dc) for dz in range(NZ) for dc in range(2)][1:]
    line.sort(key=lambda step: -hops(step[0], NZ))
    plane = [(dy, dx) for dy in range(NY) for dx in range(4)][1:]
    plane.sort(key=lambda step: -hops(step[0], NY) - hops(step[1], 4))
    line_peers = [device((z + dz) % NZ, y, x, (core + dc) % 2) for dz, dc in line]
    plane_peers = [device(z, (y + dy) % NY, (x + dx) % 4, core) for dy, dx in plane]

    load_strain = pltpu.make_async_copy(strain_hbm, strain, local_sem.at[0])
    load_strain.start()
    barrier = pltpu.get_barrier_semaphore()
    for peer in line_peers + plane_peers:
        pl.semaphore_signal(barrier, inc=1, device_id=peer, device_id_type=MESH)

    rows = pl.ds(pl.multiple_of(det * PART, PART), PART)
    loads = [
        pltpu.make_async_copy(sizes_hbm, sizes_ref, local_sem.at[3]),
        pltpu.make_async_copy(mixing_hbm.at[:, :, rows, :], mixing, local_sem.at[1]),
        pltpu.make_async_copy(filters_hbm, filters, local_sem.at[2]),
    ]
    for load in loads:
        load.start()

    padded[...] = jnp.zeros_like(padded)
    matrix = ladder_matrix()
    load_strain.wait()
    padded[:, 0:SHARD] = strain[...]
    samples = padded[...]
    high = samples.astype(BF16).astype(F32)
    middle = (samples - high).astype(BF16).astype(F32)
    low = samples - high - middle
    part = iota((8, 3 * LANES), 0)
    wide = [jnp.broadcast_to(p, (8, 3 * LANES)) for p in (high, middle, low)]
    parts = jnp.where(
        part == 0, wide[0], jnp.where(part == 1, wide[1], jnp.where(part == 2, wide[2], 0.0))
    )
    split = jnp.dot(parts.astype(BF16), matrix, preferred_element_type=F32)
    ladder = jnp.sum(split, axis=0, keepdims=True)
    row = iota((8, LANES), 0)
    lane = iota((8, LANES), 1)
    halves = [ladder[:, :LANES], ladder[:, LANES:]]
    halves += [samples[:, k * LANES : (k + 1) * LANES] for k in range(3)]
    tile = jnp.zeros((8, LANES), F32)
    for k, (r, half, first, skip, width) in enumerate(LINES):
        line = jnp.broadcast_to(halves[half], (8, LANES))
        line = jnp.where((lane >= first) & (lane < first + width), line, 0.0)
        turn = (WIDTH[r] * at_bin + skip + (LANES * 256 - START[r] - first)) % LANES
        tile = jnp.where(row == k, pltpu.roll(line, turn, 1), tile)
    own = pl.ds(pl.multiple_of((core * NZ + z) * 8, 8), 8)
    column[own, :] = tile

    pl.semaphore_wait(barrier, len(line_peers) + len(plane_peers))

    def send(ref, send_sem, recv_sem, peer):
        copy = pltpu.make_async_remote_copy(
            src_ref=ref,
            dst_ref=ref,
            send_sem=send_sem,
            recv_sem=recv_sem,
            device_id=peer,
            device_id_type=MESH,
        )
        copy.start()
        return copy

    line_copies = [
        send(column.at[own, :], line_send.at[k], line_recv.at[k], peer)
        for k, peer in enumerate(line_peers)
    ]

    for load in loads:
        load.wait()
    mix(sizes_ref, mixing, filters, bank_ref)

    for copy in line_copies:
        copy.wait_recv()
    place = y * 4 + x
    for c in range(2):
        first = c * NZ * 8
        lines = [column[pl.ds(first + k, 8, stride=8), :] for k in range(5)]
        last = column[first + 56 : first + 64, :]
        low = lines[0] + pltpu.roll(lines[0], 5, 0)
        low = low + jnp.where(row < 2, pltpu.roll(lines[0], 2, 0), 0.0)
        tail = pltpu.roll(lines[4], 5, 0) + pltpu.roll(lines[4], 4, 0)
        top = jnp.where(row < 3, low, jnp.where(row < 4, tail, lines[1]))
        bottom = jnp.where(row < 2, pltpu.roll(lines[3], 2, 0), pltpu.roll(lines[2], 5, 0))
        bottom = jnp.where(row < 5, bottom, last)
        packed = jnp.concatenate([top, bottom], axis=0)
        seen_ref[place, c] = packed.astype(BF16)

    plane_copies = [
        send(seen_ref.at[place], plane_send.at[k], plane_recv.at[k], peer)
        for k, peer in enumerate(plane_peers)
    ]
    for copy in line_copies:
        copy.wait_send()
    for copy in plane_copies:
        copy.wait_recv()
    for copy in plane_copies:
        copy.wait_send()


def begins(r, k, j):
    at, extra = k, 0
    if r == 2:
        at = k + 3
    if r == 1:
        at, extra = (k & 1) + 6, LANES * (k >> 1)
    if r == 0:
        at, extra = 7, LANES * (k - 5)
    return WIDTH[r] * (8 * at + j) + extra - START[r]


def flatten(r, seen_ref, flat):
    least, most = ROWS[r]
    row = iota((8, LANES), 0)
    lane = iota((8, LANES), 1)
    moved = [[] for _ in range(DETS)]
    for y in range(NY):
        for xh in range(NX):
            begin = begins(r, row, y * NX + xh) & (LANES - 1)
            after = lane >= begin
            before = lane < begin
            if r == 4 or r == 1:
                inside = ((lane - begin) & (LANES - 1)) < (WIDTH[4] if r == 4 else 8)
                if r == 1:
                    inside = inside | (row < 2)
                after, before = after & inside, before & inside
            for d in range(DETS):
                pair = seen_ref[y * 4 + xh * 2 + d // 2, d % 2].astype(F32)
                top, bottom = pair[:8], pair[8:]
                if r == 4:
                    block = jnp.where(row < 6, pltpu.roll(top, 3, 0), pltpu.roll(top, 6, 0))
                    block = jnp.where(row < 3, top, block)
                elif r == 1:
                    block = jnp.where(row < 2, bottom, jnp.broadcast_to(top[3:4], (8, LANES)))
                else:
                    block = top if r == 3 else bottom
                moved[d].append(jnp.where(after, block, 0.0))
                moved[d].append(jnp.where(before, block, 0.0))
    shape = (16, 2 * 8 * NY * NX)
    at = iota(shape, 1)
    k = at & 7
    where = (begins(r, k, at >> 4) >> 7) + ((at >> 3) & 1)
    pick = (where == iota(shape, 0)) & (k >= least) & (k <= most)
    data = jnp.concatenate([jnp.concatenate(m, axis=0) for m in moved], axis=1).astype(BF16)
    flat[...] = jnp.dot(pick.astype(F32).astype(BF16), data, preferred_element_type=F32)


def build_hankel(flat, hankel, blocks):
    rows = 16
    shape = (rows, LANES)
    groups = range(LANES // rows)
    later = [iota(shape, 1) > iota(shape, 0) + rows * g for g in groups]
    for d in range(DETS):
        cols = slice(d * LANES, (d + 1) * LANES)
        turned = None
        for m in range(blocks + 1):
            line = jnp.broadcast_to(flat[m : m + 1, cols], shape)
            line = pltpu.roll(line, 1, 1, stride=1, stride_axis=0).astype(BF16)
            following = [pltpu.roll(line, rows * g, 1) if g else line for g in groups]
            if m:
                for g in groups:
                    at = (m - 1) * LANES + rows * g
                    hankel[at : at + rows, cols] = jnp.where(later[g], following[g], turned[g])
            turned = following


def filter_kernel(seen_ref, bank_ref, out_hbm, flat, hankel, out, sems):
    rate = bank_ref[2 * PART :, :LANES].astype(F32).astype(jnp.int32)[0, 0]

    def total_of(snr):
        each = snr[:PART] * snr[:PART] + snr[PART:] * snr[PART:]
        total = each[:, :LANES]
        for d in range(1, DETS):
            total = total + each[:, d * LANES : (d + 1) * LANES]
        return total

    def copy_of(c):
        cols = slice(c * LANES, (c + 1) * LANES)
        return pltpu.make_async_copy(out.at[c], out_hbm.at[0, :, cols], sems.at[c])

    def write(c, value):
        out[c] = value
        copy_of(c).start()

    def finish():
        for c in range(OUT0 // LANES):
            copy_of(c).wait()

    def power(c):
        taps = hankel[c * LANES : c * LANES + TAPS, :]
        return total_of(jnp.dot(bank_ref[: 2 * PART], taps, preferred_element_type=F32))

    def repeat(total):
        high = total.astype(BF16)
        rest = total - high.astype(F32)
        middle = rest.astype(BF16)
        low = (rest - middle.astype(F32)).astype(BF16)
        shape = (total.shape[1], OUT0)
        spread = (iota(shape, 1) >> rate) == iota(shape, 0)
        spread = spread.astype(F32).astype(BF16)
        parts = jnp.concatenate([high, middle, low], axis=0)
        wide = jnp.dot(parts, spread, preferred_element_type=F32)
        wide = wide[:PART] + wide[PART : 2 * PART] + wide[2 * PART :]
        for c in range(OUT0 // LANES):
            write(c, wide[:, c * LANES : (c + 1) * LANES])
        finish()

    blocks = TAPS // LANES

    @pl.when(rate == 0)
    def _():
        flatten(0, seen_ref, flat)
        build_hankel(flat, hankel, blocks + 3)
        for c in range(OUT0 // LANES):
            write(c, power(c))
        finish()

    @pl.when(rate == 1)
    def _():
        flatten(1, seen_ref, flat)
        build_hankel(flat, hankel, blocks + 1)
        repeat(jnp.concatenate([power(0), power(1)], axis=1))

    for r in range(2, 5):

        @pl.when(rate == r)
        def _(r=r):
            flatten(r, seen_ref, flat)

    @pl.when(rate > 1)
    def _():
        build_hankel(flat, hankel, blocks)
        repeat(power(0))


def on_device(strain, filters, mixing, counts, rate_bands):
    vmem = pl.BlockSpec(memory_space=pltpu.VMEM)
    hbm = pl.BlockSpec(memory_space=pltpu.HBM)
    dma = pltpu.SemaphoreType.DMA
    given = (strain, filters, mixing)
    given = [pltpu.with_memory_space_constraint(one, pltpu.HBM) for one in given]
    params = pltpu.CompilerParams(vmem_limit_bytes=24 * 2**20)
    bank_shape = jax.ShapeDtypeStruct((2 * PART + 16, TAPS), BF16)
    bank_scratch = [pltpu.VMEM((1, KMAX, TAPS), BF16), pltpu.VMEM((1, 2, PART, KMAX), BF16)]

    at_bin = lax.axis_index("bins")
    place = 2 * jnp.minimum(at_bin >> 3, 4) + ((at_bin >> 1) & 3)
    place = place + 2 * (at_bin & 1) + (lax.axis_index("det") >> 1)
    early = place < 10

    def sizes_of(counts, rates):
        return jnp.broadcast_to(counts[0] * 8 + rates[0], (8, LANES))

    def nothing(counts, rates):
        return jnp.zeros((8, LANES), jnp.int32)

    sizes = lax.cond(early, sizes_of, nothing, counts, rate_bands)
    seen, bank = pl.pallas_call(
        gather_kernel,
        out_shape=(
            jax.ShapeDtypeStruct((NY * 4, 2, 16, LANES), BF16),
            bank_shape,
        ),
        in_specs=[hbm] * 4,
        out_specs=(vmem, vmem),
        scratch_shapes=[
            pltpu.VMEM((8, LANES), jnp.int32),
            pltpu.VMEM((1, SHARD), F32),
            pltpu.VMEM((1, 3 * LANES), F32),
            pltpu.VMEM((2 * NZ * 8, LANES), F32),
            *bank_scratch,
            dma((4,)),
            dma((2 * NZ - 1,)),
            dma((2 * NZ - 1,)),
            dma((NY * 4 - 1,)),
            dma((NY * 4 - 1,)),
        ],
        compiler_params=pltpu.CompilerParams(
            collective_id=0, has_side_effects=True, vmem_limit_bytes=24 * 2**20
        ),
        name="gather_and_mix",
    )(sizes, *given)

    def ready(bank, counts, rates, filters, mixing):
        return bank

    def late(bank, counts, rates, filters, mixing):
        return pl.pallas_call(
            mix_kernel,
            out_shape=bank_shape,
            in_specs=[vmem, hbm, hbm],
            out_specs=vmem,
            scratch_shapes=[*bank_scratch, dma((2,))],
            compiler_params=params,
            name="mix_late",
        )(sizes_of(counts, rates), filters, mixing)

    bank = lax.cond(early, ready, late, bank, counts, rate_bands, filters, mixing)
    return pl.pallas_call(
        filter_kernel,
        out_shape=jax.ShapeDtypeStruct((1, PART, OUT0), F32),
        in_specs=[vmem] * 2,
        out_specs=hbm,
        scratch_shapes=[
            pltpu.VMEM((16, DETS * LANES), F32),
            pltpu.VMEM((11 * LANES, DETS * LANES), BF16),
            pltpu.VMEM((OUT0 // LANES, PART, LANES), F32),
            dma((OUT0 // LANES,)),
        ],
        compiler_params=params,
        name="filter_and_sum",
    )(seen, bank)


def solution(mesh):
    placed = (
        P("det", "bins"),
        P("bins", None, None),
        P("bins", None, None, None),
        P("bins"),
        P("bins"),
    )
    return jax.shard_map(
        on_device, mesh=mesh, in_specs=placed, out_specs=P("bins", "det", None), check_vma=False
    )
```

```python
import jax
import jax.numpy as jnp
from jax import lax
from jax.experimental import pallas as pl
from jax.experimental.pallas import tpu as pltpu
from jax.sharding import PartitionSpec as P

DETS = 4
KMAX = 512
TAPS = 1024
TPL = 256
OUT0 = 512
SAMPLES = 17408
SHARD = 272
NZ, NY, NX = 8, 4, 2
PART = TPL // DETS
LANES = 128
MESH = pl.DeviceIdType.MESH
F32 = jnp.float32
BF16 = jnp.bfloat16
WIDTH = (272, 136, 68, 34, 17)
COLUMN = (0, 0, 136, 204, 238)
START = tuple((SAMPLES >> r) - (OUT0 >> r) - (TAPS - 1) for r in range(5))


LINES = (
    (4, 1, 110, 0, 17),
    (3, 1, 76, 0, 34),
    (2, 1, 8, 0, 68),
    (1, 0, 0, 0, 128),
    (1, 1, 0, 128, 8),
    (0, 2, 0, 0, 128),
    (0, 3, 0, 128, 128),
    (0, 4, 0, 256, 16),
)
ROWS = ((5, 7), (0, 3), (2, 4), (4, 7), (0, 7))


def iota(shape, dim):
    return lax.broadcasted_iota(jnp.int32, shape, dim)


def ladder_matrix():
    col = iota((1, 2 * LANES), 1)
    sample = iota((3 * LANES, 2 * LANES), 0)
    matrix = jnp.zeros((3 * LANES, 2 * LANES), F32)
    for r in range(1, 5):
        here = (col >= COLUMN[r]) & (col < COLUMN[r] + WIDTH[r])
        matrix = jnp.where(here & ((sample >> r) == col - COLUMN[r]), 0.5**r, matrix)
    return matrix.astype(BF16)


def hops(step, n):
    return min(step, n - step)


def mix(sizes_ref, mixing, filters, bank_ref):
    counts = jnp.concatenate([sizes_ref[0:1, :] >> 3] * (KMAX // LANES), axis=1)
    mixed = mixing[...].reshape(2 * PART, KMAX)
    mixed = jnp.where(iota((1, KMAX), 1) < counts, mixed, jnp.zeros_like(mixed))
    bank = jnp.dot(mixed, filters[0], preferred_element_type=F32).astype(BF16)
    square = (LANES, LANES)
    turn = (iota(square, 0) + iota(square, 1) == LANES - 1).astype(F32).astype(BF16)
    for a in range(TAPS // LANES):
        taps = slice(a * LANES, (a + 1) * LANES)
        turned = jnp.dot(bank[:, taps], turn, preferred_element_type=F32)
        bank_ref[: 2 * PART, taps] = turned.astype(BF16)
    rate = (sizes_ref[...] & 7).astype(F32)
    bank_ref[2 * PART :, :LANES] = jnp.concatenate([rate, rate], axis=0).astype(BF16)


def mix_kernel(sizes_ref, filters_hbm, mixing_hbm, bank_ref, filters, mixing, sems):
    rows = pl.ds(pl.multiple_of(lax.axis_index("det") * PART, PART), PART)
    loads = [
        pltpu.make_async_copy(mixing_hbm.at[:, :, rows, :], mixing, sems.at[0]),
        pltpu.make_async_copy(filters_hbm, filters, sems.at[1]),
    ]
    for load in loads:
        load.start()
    for load in loads:
        load.wait()
    mix(sizes_ref, mixing, filters, bank_ref)


def gather_kernel(
    sizes_hbm,
    strain_hbm,
    filters_hbm,
    mixing_hbm,
    seen_ref,
    bank_ref,
    sizes_ref,
    strain,
    padded,
    column,
    filters,
    mixing,
    local_sem,
    line_send,
    line_recv,
    plane_send,
    plane_recv,
):
    at_bin = lax.axis_index("bins")
    det = lax.axis_index("det")
    z = at_bin // (NY * NX)
    y = (at_bin // NX) % NY
    x = (at_bin % NX) * 2 + det // 2
    core = det % 2

    def device(z, y, x, core):
        return (z * NY + y) * NX + x // 2, (x % 2) * 2 + core

    line = [(dz, dc) for dz in range(NZ) for dc in range(2)][1:]
    line.sort(key=lambda step: -hops(step[0], NZ))
    plane = [(dy, dx) for dy in range(NY) for dx in range(4)][1:]
    plane.sort(key=lambda step: -hops(step[0], NY) - hops(step[1], 4))
    line_peers = [device((z + dz) % NZ, y, x, (core + dc) % 2) for dz, dc in line]
    plane_peers = [device(z, (y + dy) % NY, (x + dx) % 4, core) for dy, dx in plane]

    load_strain = pltpu.make_async_copy(strain_hbm, strain, local_sem.at[0])
    load_strain.start()
    barrier = pltpu.get_barrier_semaphore()
    for peer in line_peers + plane_peers:
        pl.semaphore_signal(barrier, inc=1, device_id=peer, device_id_type=MESH)

    rows = pl.ds(pl.multiple_of(det * PART, PART), PART)
    loads = [
        pltpu.make_async_copy(sizes_hbm, sizes_ref, local_sem.at[3]),
        pltpu.make_async_copy(mixing_hbm.at[:, :, rows, :], mixing, local_sem.at[1]),
        pltpu.make_async_copy(filters_hbm, filters, local_sem.at[2]),
    ]
    for load in loads:
        load.start()

    padded[...] = jnp.zeros_like(padded)
    matrix = ladder_matrix()
    load_strain.wait()
    padded[:, 0:SHARD] = strain[...]
    samples = padded[...]
    high = samples.astype(BF16).astype(F32)
    middle = (samples - high).astype(BF16).astype(F32)
    low = samples - high - middle
    part = iota((8, 3 * LANES), 0)
    wide = [jnp.broadcast_to(p, (8, 3 * LANES)) for p in (high, middle, low)]
    parts = jnp.where(
        part == 0, wide[0], jnp.where(part == 1, wide[1], jnp.where(part == 2, wide[2], 0.0))
    )
    split = jnp.dot(parts.astype(BF16), matrix, preferred_element_type=F32)
    ladder = jnp.sum(split, axis=0, keepdims=True)
    row = iota((8, LANES), 0)
    lane = iota((8, LANES), 1)
    halves = [ladder[:, :LANES], ladder[:, LANES:]]
    halves += [samples[:, k * LANES : (k + 1) * LANES] for k in range(3)]
    tile = jnp.zeros((8, LANES), F32)
    for k, (r, half, first, skip, width) in enumerate(LINES):
        line = jnp.broadcast_to(halves[half], (8, LANES))
        line = jnp.where((lane >= first) & (lane < first + width), line, 0.0)
        turn = (WIDTH[r] * at_bin + skip + (LANES * 256 - START[r] - first)) % LANES
        tile = jnp.where(row == k, pltpu.roll(line, turn, 1), tile)
    own = pl.ds(pl.multiple_of((core * NZ + z) * 8, 8), 8)
    column[own, :] = tile

    pl.semaphore_wait(barrier, len(line_peers) + len(plane_peers))

    def send(ref, send_sem, recv_sem, peer):
        copy = pltpu.make_async_remote_copy(
            src_ref=ref,
            dst_ref=ref,
            send_sem=send_sem,
            recv_sem=recv_sem,
            device_id=peer,
            device_id_type=MESH,
        )
        copy.start()
        return copy

    line_copies = [
        send(column.at[own, :], line_send.at[k], line_recv.at[k], peer)
        for k, peer in enumerate(line_peers)
    ]

    for load in loads:
        load.wait()
    mix(sizes_ref, mixing, filters, bank_ref)

    for copy in line_copies:
        copy.wait_recv()
    place = y * 4 + x
    for c in range(2):
        first = c * NZ * 8
        lines = [column[pl.ds(first + k, 8, stride=8), :] for k in range(5)]
        last = column[first + 56 : first + 64, :]
        low = lines[0] + pltpu.roll(lines[0], 5, 0)
        low = low + jnp.where(row < 2, pltpu.roll(lines[0], 2, 0), 0.0)
        tail = pltpu.roll(lines[4], 5, 0) + pltpu.roll(lines[4], 4, 0)
        top = jnp.where(row < 3, low, jnp.where(row < 4, tail, lines[1]))
        bottom = jnp.where(row < 2, pltpu.roll(lines[3], 2, 0), pltpu.roll(lines[2], 5, 0))
        bottom = jnp.where(row < 5, bottom, last)
        packed = jnp.concatenate([top, bottom], axis=0)
        seen_ref[place, c] = packed.astype(BF16)

    plane_copies = [
        send(seen_ref.at[place], plane_send.at[k], plane_recv.at[k], peer)
        for k, peer in enumerate(plane_peers)
    ]
    for copy in line_copies:
        copy.wait_send()
    for copy in plane_copies:
        copy.wait_recv()
    for copy in plane_copies:
        copy.wait_send()


def begins(r, k, j):
    at, extra = k, 0
    if r == 2:
        at = k + 3
    if r == 1:
        at, extra = (k & 1) + 6, LANES * (k >> 1)
    if r == 0:
        at, extra = 7, LANES * (k - 5)
    return WIDTH[r] * (8 * at + j) + extra - START[r]


def flatten(r, seen_ref, flat):
    least, most = ROWS[r]
    row = iota((8, LANES), 0)
    lane = iota((8, LANES), 1)
    moved = [[] for _ in range(DETS)]
    for y in range(NY):
        for xh in range(NX):
            begin = begins(r, row, y * NX + xh) & (LANES - 1)
            after = lane >= begin
            before = lane < begin
            if r == 4 or r == 1:
                inside = ((lane - begin) & (LANES - 1)) < (WIDTH[4] if r == 4 else 8)
                if r == 1:
                    inside = inside | (row < 2)
                after, before = after & inside, before & inside
            for d in range(DETS):
                pair = seen_ref[y * 4 + xh * 2 + d // 2, d % 2].astype(F32)
                top, bottom = pair[:8], pair[8:]
                if r == 4:
                    block = jnp.where(row < 6, pltpu.roll(top, 3, 0), pltpu.roll(top, 6, 0))
                    block = jnp.where(row < 3, top, block)
                elif r == 1:
                    block = jnp.where(row < 2, bottom, jnp.broadcast_to(top[3:4], (8, LANES)))
                else:
                    block = top if r == 3 else bottom
                moved[d].append(jnp.where(after, block, 0.0))
                moved[d].append(jnp.where(before, block, 0.0))
    shape = (16, 2 * 8 * NY * NX)
    at = iota(shape, 1)
    k = at & 7
    where = (begins(r, k, at >> 4) >> 7) + ((at >> 3) & 1)
    pick = (where == iota(shape, 0)) & (k >= least) & (k <= most)
    data = jnp.concatenate([jnp.concatenate(m, axis=0) for m in moved], axis=1).astype(BF16)
    flat[...] = jnp.dot(pick.astype(F32).astype(BF16), data, preferred_element_type=F32)


def build_hankel(flat, hankel, blocks):
    rows = 16
    shape = (rows, LANES)
    groups = range(LANES // rows)
    later = [iota(shape, 1) > iota(shape, 0) + rows * g for g in groups]
    for d in range(DETS):
        cols = slice(d * LANES, (d + 1) * LANES)
        turned = None
        for m in range(blocks + 1):
            line = jnp.broadcast_to(flat[m : m + 1, cols], shape)
            line = pltpu.roll(line, 1, 1, stride=1, stride_axis=0).astype(BF16)
            following = [pltpu.roll(line, rows * g, 1) if g else line for g in groups]
            if m:
                for g in groups:
                    at = (m - 1) * LANES + rows * g
                    hankel[at : at + rows, cols] = jnp.where(later[g], following[g], turned[g])
            turned = following


def filter_kernel(seen_ref, bank_ref, out_hbm, flat, hankel, out, sems):
    rate = bank_ref[2 * PART :, :LANES].astype(F32).astype(jnp.int32)[0, 0]

    def total_of(snr):
        each = snr[:PART] * snr[:PART] + snr[PART:] * snr[PART:]
        total = each[:, :LANES]
        for d in range(1, DETS):
            total = total + each[:, d * LANES : (d + 1) * LANES]
        return total

    def copy_of(c):
        cols = slice(c * LANES, (c + 1) * LANES)
        return pltpu.make_async_copy(out.at[c], out_hbm.at[0, :, cols], sems.at[c])

    def write(c, value):
        out[c] = value
        copy_of(c).start()

    def finish():
        for c in range(OUT0 // LANES):
            copy_of(c).wait()

    def power(c):
        taps = hankel[c * LANES : c * LANES + TAPS, :]
        return total_of(jnp.dot(bank_ref[: 2 * PART], taps, preferred_element_type=F32))

    def repeat(total):
        high = total.astype(BF16)
        rest = total - high.astype(F32)
        middle = rest.astype(BF16)
        low = (rest - middle.astype(F32)).astype(BF16)
        shape = (total.shape[1], OUT0)
        spread = (iota(shape, 1) >> rate) == iota(shape, 0)
        spread = spread.astype(F32).astype(BF16)
        parts = jnp.concatenate([high, middle, low], axis=0)
        wide = jnp.dot(parts, spread, preferred_element_type=F32)
        wide = wide[:PART] + wide[PART : 2 * PART] + wide[2 * PART :]
        for c in range(OUT0 // LANES):
            write(c, wide[:, c * LANES : (c + 1) * LANES])
        finish()

    blocks = TAPS // LANES

    @pl.when(rate == 0)
    def _():
        flatten(0, seen_ref, flat)
        build_hankel(flat, hankel, blocks + 3)
        for c in range(OUT0 // LANES):
            write(c, power(c))
        finish()

    @pl.when(rate == 1)
    def _():
        flatten(1, seen_ref, flat)
        build_hankel(flat, hankel, blocks + 1)
        repeat(jnp.concatenate([power(0), power(1)], axis=1))

    for r in range(2, 5):

        @pl.when(rate == r)
        def _(r=r):
            flatten(r, seen_ref, flat)

    @pl.when(rate > 1)
    def _():
        build_hankel(flat, hankel, blocks)
        repeat(power(0))


def on_device(strain, filters, mixing, counts, rate_bands):
    vmem = pl.BlockSpec(memory_space=pltpu.VMEM)
    hbm = pl.BlockSpec(memory_space=pltpu.HBM)
    dma = pltpu.SemaphoreType.DMA
    given = (strain, filters, mixing)
    given = [pltpu.with_memory_space_constraint(one, pltpu.HBM) for one in given]
    params = pltpu.CompilerParams(vmem_limit_bytes=24 * 2**20)
    bank_shape = jax.ShapeDtypeStruct((2 * PART + 16, TAPS), BF16)
    bank_scratch = [pltpu.VMEM((1, KMAX, TAPS), BF16), pltpu.VMEM((1, 2, PART, KMAX), BF16)]

    at_bin = lax.axis_index("bins")
    place = 2 * jnp.minimum(at_bin >> 3, 4) + ((at_bin >> 1) & 3)
    place = place + 2 * (at_bin & 1) + (lax.axis_index("det") >> 1)
    early = place < 9

    def sizes_of(counts, rates):
        return jnp.broadcast_to(counts[0] * 8 + rates[0], (8, LANES))

    def nothing(counts, rates):
        return jnp.zeros((8, LANES), jnp.int32)

    sizes = lax.cond(early, sizes_of, nothing, counts, rate_bands)
    seen, bank = pl.pallas_call(
        gather_kernel,
        out_shape=(
            jax.ShapeDtypeStruct((NY * 4, 2, 16, LANES), BF16),
            bank_shape,
        ),
        in_specs=[hbm] * 4,
        out_specs=(vmem, vmem),
        scratch_shapes=[
            pltpu.VMEM((8, LANES), jnp.int32),
            pltpu.VMEM((1, SHARD), F32),
            pltpu.VMEM((1, 3 * LANES), F32),
            pltpu.VMEM((2 * NZ * 8, LANES), F32),
            *bank_scratch,
            dma((4,)),
            dma((2 * NZ - 1,)),
            dma((2 * NZ - 1,)),
            dma((NY * 4 - 1,)),
            dma((NY * 4 - 1,)),
        ],
        compiler_params=pltpu.CompilerParams(
            collective_id=0, has_side_effects=True, vmem_limit_bytes=24 * 2**20
        ),
        name="gather_and_mix",
    )(sizes, *given)

    def ready(bank, counts, rates, filters, mixing):
        return bank

    def late(bank, counts, rates, filters, mixing):
        return pl.pallas_call(
            mix_kernel,
            out_shape=bank_shape,
            in_specs=[vmem, hbm, hbm],
            out_specs=vmem,
            scratch_shapes=[*bank_scratch, dma((2,))],
            compiler_params=params,
            name="mix_late",
        )(sizes_of(counts, rates), filters, mixing)

    bank = lax.cond(early, ready, late, bank, counts, rate_bands, filters, mixing)
    return pl.pallas_call(
        filter_kernel,
        out_shape=jax.ShapeDtypeStruct((1, PART, OUT0), F32),
        in_specs=[vmem] * 2,
        out_specs=hbm,
        scratch_shapes=[
            pltpu.VMEM((16, DETS * LANES), F32),
            pltpu.VMEM((11 * LANES, DETS * LANES), BF16),
            pltpu.VMEM((OUT0 // LANES, PART, LANES), F32),
            dma((OUT0 // LANES,)),
        ],
        compiler_params=params,
        name="filter_and_sum",
    )(seen, bank)


def solution(mesh):
    placed = (
        P("det", "bins"),
        P("bins", None, None),
        P("bins", None, None, None),
        P("bins"),
        P("bins"),
    )
    return jax.shard_map(
        on_device, mesh=mesh, in_specs=placed, out_specs=P("bins", "det", None), check_vma=False
    )
```
